32 devices in a mesh: ka: 4 (over y, x), kp: 8 (over z, core).
Axes of the slice: x: 2, y: 2, z: 4, core: 2. Of those that a mesh axis runs over, the one named last changes fastest.
Arguments:
- waves: bfloat16 [8, 16, 4096], P('ka', None, 'kp'), may hold values from -6 to 6
- screen: float32 [8, 512], replicated, may hold values from 0.1 to 2
- pair_table: int32 [8, 8], P('ka', 'kp'), may hold values from 0 to 7
- plane_map: int32 [512], replicated, may hold values from 1 to 4095, as said below
- trial: bfloat16 [8, 64, 128], P('kp', None, 'ka'), may hold values from -6 to 6
- probe: bfloat16 [8, 64, 128], P('ka', None, 'kp'), may hold values from -6 to 6
Outputs:
- applied: float32 [8, 64, 128], P('ka', None, 'kp')
- adjoint: float32 [8, 64, 128], P('kp', None, 'ka')
The draws below stay inside these ranges and needn't reach their ends.
Inputs may be any that keep to these rules, and one draw needn't show every extreme that they name: `plane_map`: the 512 values are distinct and none is 0.
All inputs are finite; a program needn't handle non-finite values.
Results may differ from the reference program's by a relative error of at most 0.0003.
Values may be sent and summed in bfloat16 or wider, within the bound.
A program may use at most 64 MiB of HBM per device.

```python
import math
import jax
import jax.numpy as jnp
from jax import lax

NV = 8
NC = 8
NR = 4096
NG = 512
M = 128
NK = 8


def draw_plane_map(key, part):
    return (jax.random.permutation(key, NR - 1)[:NG] + 1).astype(jnp.int32)


def place_ends(values, rng, low, top_value):
    spot = [jax.random.randint(jax.random.fold_in(rng, axis), (), 0, length) for axis, length in enumerate(values.shape)]
    main_axis = values.shape.index(max(values.shape))
    neighbour = spot[:main_axis] + [(spot[main_axis] + 1) % values.shape[main_axis]] + spot[main_axis + 1:]
    return values.at[tuple(spot)].set(low).at[tuple(neighbour)].set(top_value)


def shard_levels(own_key, dims, cuts, smallest, high):
    factor_of, own = 1.0, jax.random.fold_in(own_key, 6)
    for position, blocks in cuts:
        steps = jnp.exp(jax.random.uniform(jax.random.fold_in(own, position), (blocks,), jnp.float32, smallest / len(cuts), high / len(cuts)))
        factor_of = factor_of * jnp.repeat(steps, dims[position] // blocks).reshape([-1 if axis == position else 1 for axis in range(len(dims))])
    return factor_of


def noise(own_key, extent, spread, most, cuts=(), kind=jnp.bfloat16):
    factor_of = shard_levels(own_key, extent, cuts, -0.22, 0.18) if cuts else 1.0
    result = jax.random.normal(own_key, extent, jnp.float32) * spread * factor_of
    return jnp.minimum(jnp.maximum(result, -most), most).astype(kind)


def setup_inputs(seed: int = 0) -> dict:
    key_of = jax.random.split(jax.random.key(seed), 7)
    waves = noise(key_of[0], (NK, NV + NC, NR), 1.0, 6.0, ((0, 4), (2, 8)))
    screen = jnp.clip(jnp.exp(jax.random.uniform(key_of[1], (NK, NG), jnp.float32, math.log(0.1), math.log(2.0))), 0.1, 2.0)
    pair_table = place_ends(jax.random.randint(key_of[2], (NK, NK), 0, NK), jax.random.fold_in(key_of[2], 1), 0, NK - 1).astype(jnp.int32)
    plane_map = draw_plane_map(jax.random.fold_in(key_of[6], 71), 0)
    trial = noise(key_of[4], (NK, NV * NC, M), 1.0, 6.0, ((0, 8), (2, 4)))
    probe = noise(key_of[5], (NK, NV * NC, M), 1.0, 6.0, ((0, 4), (2, 8)))
    return {"waves": waves, "screen": screen, "pair_table": pair_table, "plane_map": plane_map, "trial": trial, "probe": probe}


def reference(waves, screen, pair_table, plane_map, trial, probe):
    total_k = waves.shape[0]
    width = NV * NC
    scale = NR ** -0.5

    def block(pair_index):
        first = pair_index // total_k
        second = pair_index % total_k
        left = lax.dynamic_index_in_dim(waves, first, 0, keepdims=False).astype(jnp.float32)
        right = lax.dynamic_index_in_dim(waves, second, 0, keepdims=False).astype(jnp.float32)
        valence = left[:NV, None, :] * right[None, :NV, :]
        conduction = left[NV:, None, :] * right[None, NV:, :]
        vspec = jnp.fft.fft(valence, axis=-1)[..., plane_map] * scale
        cspec = jnp.fft.fft(conduction, axis=-1)[..., plane_map] * scale
        weight = screen[pair_table[first, second]]
        kernel = jnp.einsum("xyg,uwg->uxwy", jnp.real(cspec) * weight, jnp.real(vspec), precision=lax.Precision.HIGHEST)
        kernel = kernel + jnp.einsum("xyg,uwg->uxwy", jnp.imag(cspec) * weight, jnp.imag(vspec), precision=lax.Precision.HIGHEST)
        return (kernel / NG).reshape(width, width)

    blocks = lax.map(block, jnp.arange(total_k * total_k, dtype=jnp.int32))
    blocks = blocks.reshape(total_k, total_k, width, width)
    applied = jnp.einsum("kjab,jbm->kam", blocks, trial.astype(jnp.float32), precision=lax.Precision.HIGHEST)
    adjoint = jnp.einsum("kjab,kam->jbm", blocks, probe.astype(jnp.float32), precision=lax.Precision.HIGHEST)
    return applied, adjoint
```

```python
import functools
import math

import jax
import jax.numpy as jnp
import numpy as np
from jax import lax
from jax.experimental import pallas as pl
from jax.experimental.pallas import tpu as pltpu
from jax.sharding import PartitionSpec as P

NV = 8
NC = 8
LANES = 128
MESH = pl.DeviceIdType.MESH
NT = (((1,), (1,)), ((), ()))
NN = (((1,), (0,)), ((), ()))


def split(value):
    high = value.astype(jnp.bfloat16)
    low = (value - high.astype(jnp.float32)).astype(jnp.bfloat16)
    return high, low


def dot(left, right, dims=NN):
    return lax.dot_general(left, right, dims, preferred_element_type=jnp.float32)


def real_dft(values):
    n = len(values)
    if n == 1:
        return [(values[0], None)]
    if n == 2:
        return [(values[0] + values[1], None), (values[0] - values[1], None)]
    even = real_dft(values[0::2])
    odd = real_dft(values[1::2])
    out = [None] * (n // 2 + 1)
    for k in range(n // 4 + 1):
        e_re, e_im = even[k]
        o_re, o_im = odd[k]
        if k == 0:
            out[0] = (e_re + o_re, None)
            out[n // 2] = (e_re - o_re, None)
            continue
        if 4 * k == n:
            out[k] = (e_re, -o_re)
            continue
        c = math.cos(2.0 * math.pi * k / n)
        s = math.sin(2.0 * math.pi * k / n)
        if 8 * k == n and o_im is not None:
            t_re, t_im = (o_re + o_im) * c, (o_im - o_re) * c
        elif o_im is None:
            t_re, t_im = o_re * c, o_re * (-s)
        else:
            t_re, t_im = o_re * c + o_im * s, o_im * c - o_re * s
        if e_im is None:
            out[k] = (e_re + t_re, t_im)
            out[n // 2 - k] = (e_re - t_re, t_im)
        else:
            out[k] = (e_re + t_re, e_im + t_im)
            out[n // 2 - k] = (e_re - t_re, t_im - e_im)
    return out


def make_tables(outer, inner):
    base = np.arange(inner)
    phase = 2.0 * np.pi * ((base[:, None] * base[None, :]) % inner) / inner
    cos, sin = np.cos(phase), np.sin(phase)
    full = np.block([[cos, -sin], [sin, cos]]).astype(np.float32)
    high = full.astype(jnp.bfloat16)
    low = (full - high.astype(np.float32)).astype(jnp.bfloat16)
    half = np.arange(outer // 2 + 1)
    phase = 2.0 * np.pi * (half[:, None] * base[None, :]) / (outer * inner)
    twist = np.stack([np.cos(phase), np.sin(phase)], axis=1).astype(np.float32)
    return np.stack([high, low]), twist.reshape(2 * (outer // 2 + 1), inner)


def kernel(
    n_ka,
    n_kp,
    waves_ref,
    screen_ref,
    table_ref,
    plane_ref,
    trial_ref,
    probe_ref,
    dft_ref,
    twist_ref,
    applied_ref,
    adjoint_ref,
    rows,
    cols,
    trials,
    probes,
    left_f,
    right_f,
    weights,
    stage,
    blocks,
    trial_f,
    probe_f,
    app_send,
    app_recv,
    adj_send,
    adj_recv,
    row_sems,
    col_sems,
    trial_sems,
    probe_sems,
    app_sems,
    adj_sems,
    col_out_sems,
):
    a = lax.axis_index("ka")
    b = lax.axis_index("kp")
    k_rows, bands, part = waves_ref.shape
    points = part * n_kp
    inner = LANES
    outer = points // inner
    half = outer // 2 + 1
    planes = plane_ref.shape[1]
    width = NV * NC
    source = b // k_rows
    foreign = source != a

    barrier = pltpu.get_barrier_semaphore()

    def greet(to_a, to_b):
        pl.semaphore_signal(barrier, inc=1, device_id=(to_a, to_b), device_id_type=MESH)

    def kp_peer(step):
        return lax.rem(b + step, n_kp)

    def ka_peer(step):
        return lax.rem(a + step, n_ka)

    for step in range(1, n_kp):
        greet(a, kp_peer(step))
    for step in range(1, n_ka):
        greet(ka_peer(step), b)
        for t in range(k_rows):
            greet(ka_peer(step), a * k_rows + t)

    @pl.when(foreign)
    def _():
        for step in range(n_kp):
            greet(source, kp_peer(step))

    fixed = (n_kp - 1) + (n_ka - 1) * (1 + k_rows)
    pl.semaphore_wait(barrier, fixed + jnp.where(foreign, n_kp, 0))

    def remote(src, dst, send, recv, to_a, to_b):
        return pltpu.make_async_remote_copy(
            src_ref=src,
            dst_ref=dst,
            send_sem=send,
            recv_sem=recv,
            device_id=(to_a, to_b),
            device_id_type=MESH,
        )

    sends = []
    for step in range(1, n_kp):
        sends.append(
            remote(waves_ref, rows.at[b], row_sems.at[0, step], row_sems.at[1, b], a, kp_peer(step))
        )
    for step in range(1, n_ka):
        for t in range(k_rows):
            sends.append(
                remote(
                    waves_ref.at[t],
                    cols.at[b],
                    col_out_sems.at[step, t],
                    col_sems.at[b],
                    ka_peer(step),
                    a * k_rows + t,
                )
            )
    for step in range(1, n_ka):
        sends.append(
            remote(trial_ref, trials.at[a], trial_sems.at[0, step], trial_sems.at[1, a], ka_peer(step), b)
        )
    for step in range(1, n_kp):
        sends.append(
            remote(probe_ref, probes.at[b], probe_sems.at[0, step], probe_sems.at[1, b], a, kp_peer(step))
        )
    for copy in sends:
        copy.start()

    rows[b] = waves_ref[...]
    trials[a] = trial_ref[...]
    probes[b] = probe_ref[...]

    plane = plane_ref[...]
    first = jnp.bitwise_and(plane, outer - 1)
    plane = jnp.where(first > outer // 2, points - plane, plane)
    first = jnp.bitwise_and(plane, outer - 1)
    second = jnp.right_shift(plane, int(math.log2(outer)))
    pad = weights.shape[1]
    one_first = lax.broadcasted_iota(jnp.int32, (pad, planes), 0) == first
    one_second = (lax.broadcasted_iota(jnp.int32, (inner, planes), 0) == second).astype(jnp.float32)
    screen = screen_ref[...]
    scale = 1.0 / (points * planes)
    for p in range(k_rows):
        chosen = lax.broadcasted_iota(jnp.int32, screen.shape, 0) == table_ref[p, 0]
        line = jnp.sum(jnp.where(chosen, screen, 0.0), axis=0, keepdims=True) * scale
        weights[p] = lax.dot_general(
            jnp.where(one_first, line, 0.0),
            one_second,
            NT,
            precision=lax.Precision.HIGHEST,
            preferred_element_type=jnp.float32,
        )

    for step in range(1, n_kp):
        peer = kp_peer(step)
        remote(waves_ref, rows.at[peer], row_sems.at[0, step], row_sems.at[1, peer], a, peer).wait_recv()

    @pl.when(foreign)
    def _():
        for step in range(n_kp):
            peer = kp_peer(step)
            remote(
                waves_ref.at[0], cols.at[peer], col_out_sems.at[0, 0], col_sems.at[peer], source, peer
            ).wait_recv()
        for i in range(n_kp):
            right_f[:, :, i * part : (i + 1) * part] = (
                cols[i].astype(jnp.float32).reshape(2, NV, part)
            )

    @pl.when(jnp.logical_not(foreign))
    def _():
        own = b - source * k_rows
        for i in range(n_kp):
            right_f[:, :, i * part : (i + 1) * part] = (
                rows[i, own].astype(jnp.float32).reshape(2, NV, part)
            )

    for i in range(n_kp):
        for p in range(k_rows):
            left_f[2 * p : 2 * p + 2, :, i * part : (i + 1) * part] = (
                rows[i, p].astype(jnp.float32).reshape(2, NV, part)
            )

    def first_stage(group, carry):
        kind = lax.rem(group, 2)
        for u in range(NV):
            values = []
            for r in range(outer):
                lanes = slice(r * inner, (r + 1) * inner)
                values.append(left_f[group, u : u + 1, lanes] * right_f[kind, :, lanes])
            spots = pl.ds(pl.multiple_of((group * NV + u) * NV, NV), NV)
            for f, (re, im) in enumerate(real_dft(values)):
                if f == 0:
                    stage[f, spots, :inner] = re
                    stage[f, spots, inner:] = jnp.zeros_like(re)
                    continue
                c = twist_ref[2 * f : 2 * f + 1, :]
                s = twist_ref[2 * f + 1 : 2 * f + 2, :]
                if im is None:
                    stage[f, spots, :inner] = re * c
                    stage[f, spots, inner:] = -(re * s)
                else:
                    stage[f, spots, :inner] = re * c + im * s
                    stage[f, spots, inner:] = im * c - re * s
        return carry

    lax.fori_loop(0, 2 * k_rows, first_stage, 0)

    dft_high = dft_ref[0]
    dft_low = dft_ref[1]
    both = 2 * width

    def second_stage(f, sums):
        high, low = split(stage[f])
        spec = dot(high, dft_high) + (dot(low, dft_high) + dot(high, dft_low))
        out = []
        for p in range(k_rows):
            line = weights[p, pl.ds(f, 1), :]
            line = jnp.concatenate([line, line], axis=1)
            val = spec[p * both : p * both + width]
            con = spec[p * both + width : (p + 1) * both] * line
            left = jnp.concatenate(split(val), axis=0)
            right = jnp.concatenate(split(con), axis=0)
            out.append(sums[p] + dot(left, right, NT))
        return tuple(out)

    zero = jnp.zeros((both, both), jnp.float32)
    sums = lax.fori_loop(0, half, second_stage, (zero,) * k_rows)
    for p in range(k_rows):
        total = sums[p][:width] + sums[p][width:]
        blocks[p * width : (p + 1) * width, :] = total + pltpu.roll(total, width, 1)

    grid = blocks[...]
    row_id = lax.broadcasted_iota(jnp.int32, grid.shape, 0)
    lane_id = lax.broadcasted_iota(jnp.int32, grid.shape, 1) // NC
    n_rows, n_lanes = grid.shape
    bit = 1
    while bit < NV:
        row_bit = jnp.bitwise_and(row_id, bit)
        lane_bit = jnp.bitwise_and(lane_id, bit)
        down = pltpu.roll(pltpu.roll(grid, n_rows - bit, 0), bit * NC, 1)
        up = pltpu.roll(pltpu.roll(grid, bit, 0), n_lanes - bit * NC, 1)
        grid = jnp.where(row_bit == lane_bit, grid, jnp.where(row_bit == 0, down, up))
        bit *= 2

    for step in range(1, n_ka):
        peer = ka_peer(step)
        remote(trial_ref, trials.at[peer], trial_sems.at[0, step], trial_sems.at[1, peer], peer, b).wait_recv()
    for step in range(1, n_kp):
        peer = kp_peer(step)
        remote(probe_ref, probes.at[peer], probe_sems.at[0, step], probe_sems.at[1, peer], a, peer).wait_recv()
    m_ka = trial_ref.shape[0]
    m_kp = probe_ref.shape[0]
    for i in range(n_ka):
        trial_f[i * m_ka : (i + 1) * m_ka, :] = trials[i].astype(jnp.float32)
    for i in range(n_kp):
        probe_f[i * m_kp : (i + 1) * m_kp, :] = probes[i].astype(jnp.float32)

    grid_high, grid_low = split(grid)
    trial = trial_f[...].astype(jnp.bfloat16)
    probe = probe_f[...].astype(jnp.bfloat16)
    forward = dot(trial, grid_high[:, :width], NT) + dot(trial, grid_low[:, :width], NT)
    backward = (dot(probe, grid_high) + dot(probe, grid_low))[:, :width]
    for i in range(n_kp):
        app_send[i] = forward[i * m_kp : (i + 1) * m_kp]
    for i in range(n_ka):
        adj_send[i] = backward[i * m_ka : (i + 1) * m_ka]

    outs = []
    for step in range(1, n_kp):
        peer = kp_peer(step)
        outs.append(
            remote(app_send.at[peer], app_recv.at[b], app_sems.at[0, step], app_sems.at[1, b], a, peer)
        )
    for step in range(1, n_ka):
        peer = ka_peer(step)
        outs.append(
            remote(adj_send.at[peer], adj_recv.at[a], adj_sems.at[0, step], adj_sems.at[1, a], peer, b)
        )
    for copy in outs:
        copy.start()
    total = app_send[b]
    for step in range(1, n_kp):
        peer = kp_peer(step)
        remote(
            app_send.at[peer], app_recv.at[peer], app_sems.at[0, step], app_sems.at[1, peer], a, peer
        ).wait_recv()
        total = total + app_recv[peer]
    applied_ref[...] = total
    total = adj_send[a]
    for step in range(1, n_ka):
        peer = ka_peer(step)
        remote(
            adj_send.at[peer], adj_recv.at[peer], adj_sems.at[0, step], adj_sems.at[1, peer], peer, b
        ).wait_recv()
        total = total + adj_recv[peer]
    adjoint_ref[...] = total
    for copy in sends + outs:
        copy.wait_send()


def shards(n_ka, n_kp, waves, screen, pair_table, plane_map, trial, probe):
    k_rows, bands, part = waves.shape
    width = NV * NC
    points = part * n_kp
    outer = points // LANES
    half = outer // 2 + 1
    pad = -(-half // 8) * 8
    m_ka = trial.shape[2]
    m_kp = probe.shape[2]
    columns = m_ka * n_ka
    dft, twist = make_tables(outer, LANES)
    trial_t = trial.reshape(width, m_ka).T
    probe_t = probe.reshape(k_rows * width, m_kp).T
    f32, bf16 = jnp.float32, jnp.bfloat16
    vmem = pl.BlockSpec(memory_space=pltpu.VMEM)
    smem = pl.BlockSpec(memory_space=pltpu.SMEM)
    dma = pltpu.SemaphoreType.DMA
    applied, adjoint = pl.pallas_call(
        functools.partial(kernel, n_ka, n_kp),
        out_shape=(
            jax.ShapeDtypeStruct((m_kp, k_rows * width), f32),
            jax.ShapeDtypeStruct((m_ka, width), f32),
        ),
        in_specs=[vmem, vmem, smem, vmem, vmem, vmem, vmem, vmem],
        out_specs=(vmem, vmem),
        scratch_shapes=[
            pltpu.VMEM((n_kp, k_rows, bands, part), bf16),
            pltpu.VMEM((n_kp, bands, part), bf16),
            pltpu.VMEM((n_ka, m_ka, width), bf16),
            pltpu.VMEM((n_kp, m_kp, k_rows * width), bf16),
            pltpu.VMEM((2 * k_rows, NV, points), f32),
            pltpu.VMEM((2, NV, points), f32),
            pltpu.VMEM((k_rows, pad, LANES), f32),
            pltpu.VMEM((half, k_rows * 2 * width, 2 * LANES), f32),
            pltpu.VMEM((k_rows * width, 2 * width), f32),
            pltpu.VMEM((columns, width), f32),
            pltpu.VMEM((columns, k_rows * width), f32),
            pltpu.VMEM((n_kp, m_kp, k_rows * width), f32),
            pltpu.VMEM((n_kp, m_kp, k_rows * width), f32),
            pltpu.VMEM((n_ka, m_ka, width), f32),
            pltpu.VMEM((n_ka, m_ka, width), f32),
            dma((2, n_kp)),
            dma((n_kp,)),
            dma((2, n_ka)),
            dma((2, n_kp)),
            dma((2, n_kp)),
            dma((2, n_ka)),
            dma((n_ka, k_rows)),
        ],
        compiler_params=pltpu.CompilerParams(
            collective_id=0, has_side_effects=True, vmem_limit_bytes=60000 * 1024
        ),
    )(
        waves,
        screen,
        pair_table,
        plane_map.reshape(1, -1),
        trial_t,
        probe_t,
        jnp.asarray(dft),
        jnp.asarray(twist),
    )
    applied = applied.T.reshape(k_rows, width, m_kp)
    adjoint = adjoint.T.reshape(1, width, m_ka)
    return (applied, adjoint)


def solution(mesh):
    placed = (
        P("ka", None, "kp"),
        P(),
        P("ka", "kp"),
        P(),
        P("kp", None, "ka"),
        P("ka", None, "kp"),
    )
    return jax.shard_map(
        functools.partial(shards, mesh.shape["ka"], mesh.shape["kp"]),
        mesh=mesh,
        in_specs=placed,
        out_specs=(P("ka", None, "kp"), P("kp", None, "ka")),
        check_vma=False,
    )
```

```python
import functools
import math

import jax
import jax.numpy as jnp
import numpy as np
from jax import lax
from jax.experimental import pallas as pl
from jax.experimental.pallas import tpu as pltpu
from jax.sharding import PartitionSpec as P

NV = 8
NC = 8
LANES = 128
MESH = pl.DeviceIdType.MESH
NT = (((1,), (1,)), ((), ()))
NN = (((1,), (0,)), ((), ()))


def split(value):
    high = value.astype(jnp.bfloat16)
    low = (value - high.astype(jnp.float32)).astype(jnp.bfloat16)
    return high, low


def dot(left, right, dims=NN):
    return lax.dot_general(left, right, dims, preferred_element_type=jnp.float32)


def real_dft(values):
    n = len(values)
    if n == 1:
        return [(values[0], None)]
    if n == 2:
        return [(values[0] + values[1], None), (values[0] - values[1], None)]
    even = real_dft(values[0::2])
    odd = real_dft(values[1::2])
    out = [None] * (n // 2 + 1)
    for k in range(n // 4 + 1):
        e_re, e_im = even[k]
        o_re, o_im = odd[k]
        if k == 0:
            out[0] = (e_re + o_re, None)
            out[n // 2] = (e_re - o_re, None)
            continue
        if 4 * k == n:
            out[k] = (e_re, -o_re)
            continue
        c = math.cos(2.0 * math.pi * k / n)
        s = math.sin(2.0 * math.pi * k / n)
        if 8 * k == n and o_im is not None:
            t_re, t_im = (o_re + o_im) * c, (o_im - o_re) * c
        elif o_im is None:
            t_re, t_im = o_re * c, o_re * (-s)
        else:
            t_re, t_im = o_re * c + o_im * s, o_im * c - o_re * s
        if e_im is None:
            out[k] = (e_re + t_re, t_im)
            out[n // 2 - k] = (e_re - t_re, t_im)
        else:
            out[k] = (e_re + t_re, e_im + t_im)
            out[n // 2 - k] = (e_re - t_re, t_im - e_im)
    return out


def make_tables(outer, inner):
    base = np.arange(inner)
    phase = 2.0 * np.pi * ((base[:, None] * base[None, :]) % inner) / inner
    cos, sin = np.cos(phase), np.sin(phase)
    full = np.block([[cos, -sin], [sin, cos]]).astype(np.float32)
    high = full.astype(jnp.bfloat16)
    low = (full - high.astype(np.float32)).astype(jnp.bfloat16)
    half = np.arange(outer // 2 + 1)
    phase = 2.0 * np.pi * (half[:, None] * base[None, :]) / (outer * inner)
    twist = np.stack([np.cos(phase), np.sin(phase)], axis=1).astype(np.float32)
    return np.stack([high, low]), twist.reshape(2 * (outer // 2 + 1), inner)


def kernel(
    n_ka,
    n_kp,
    waves_ref,
    screen_ref,
    table_ref,
    plane_ref,
    trial_ref,
    probe_ref,
    dft_ref,
    twist_ref,
    applied_ref,
    adjoint_ref,
    slabs,
    rows,
    cols,
    trials,
    probes,
    left_f,
    right_f,
    weights,
    stage,
    blocks,
    trial_f,
    probe_f,
    app_send,
    app_recv,
    adj_send,
    adj_recv,
    own_sems,
    slab_sems,
    row_sems,
    col_sems,
    trial_sems,
    probe_sems,
    app_sems,
    adj_sems,
):
    a = lax.axis_index("ka")
    b = lax.axis_index("kp")
    k_rows, bands, part = waves_ref.shape
    points = part * n_kp
    inner = LANES
    outer = points // inner
    half = outer // 2 + 1
    planes = plane_ref.shape[1]
    width = NV * NC
    both = 2 * width

    barrier = pltpu.get_barrier_semaphore()

    def greet(to_a, to_b):
        pl.semaphore_signal(barrier, inc=1, device_id=(to_a, to_b), device_id_type=MESH)

    def kp_peer(step):
        return lax.rem(b + step, n_kp)

    def ka_peer(step):
        return lax.rem(a + step, n_ka)

    for step in range(1, n_kp):
        greet(a, kp_peer(step))
    for step in range(1, n_ka):
        greet(ka_peer(step), b)
    own_slab = pltpu.make_async_copy(waves_ref, slabs.at[a], own_sems.at[0])
    own_slab.start()
    own_slab.wait()
    own_col = pltpu.make_async_copy(waves_ref, rows.at[b], own_sems.at[1])
    own_col.start()
    own_col.wait()
    trials[a] = trial_ref[...]
    probes[b] = probe_ref[...]
    pl.semaphore_wait(barrier, (n_kp - 1) + (n_ka - 1))

    def remote(src, dst, send, recv, to_a, to_b):
        return pltpu.make_async_remote_copy(
            src_ref=src,
            dst_ref=dst,
            send_sem=send,
            recv_sem=recv,
            device_id=(to_a, to_b),
            device_id_type=MESH,
        )

    def slab_copy(step, slot):
        return remote(
            waves_ref, slabs.at[slot], slab_sems.at[0, step], slab_sems.at[1, slot], ka_peer(step), b
        )

    def row_copy(step, p, slot):
        return remote(
            waves_ref.at[p],
            rows.at[slot, p],
            row_sems.at[0, step, p],
            row_sems.at[1, slot, p],
            a,
            kp_peer(step),
        )

    def col_copy(step, slot):
        peer = kp_peer(step)
        return remote(
            slabs.at[peer // k_rows, lax.rem(peer, k_rows)],
            cols.at[slot],
            col_sems.at[0, step],
            col_sems.at[1, slot],
            a,
            peer,
        )

    def trial_copy(step, slot):
        return remote(
            trial_ref, trials.at[slot], trial_sems.at[0, step], trial_sems.at[1, slot], ka_peer(step), b
        )

    def probe_copy(step, slot):
        return remote(
            probe_ref, probes.at[slot], probe_sems.at[0, step], probe_sems.at[1, slot], a, kp_peer(step)
        )

    sends = []

    def send(copy):
        copy.start()
        sends.append(copy)

    for step in range(1, n_ka):
        send(slab_copy(step, a))
    for step in range(1, n_kp):
        send(row_copy(step, 0, b))
    for step in range(1, n_ka):
        slab_copy(step, ka_peer(step)).wait_recv()
    for step in range(1, n_kp):
        send(col_copy(step, b))
    for p in range(1, k_rows):
        for step in range(1, n_kp):
            send(row_copy(step, p, b))
    for step in range(1, n_ka):
        send(trial_copy(step, a))
    for step in range(1, n_kp):
        send(probe_copy(step, b))
    own_col = pltpu.make_async_copy(
        slabs.at[b // k_rows, lax.rem(b, k_rows)], cols.at[b], own_sems.at[2]
    )
    own_col.start()
    own_col.wait()

    plane = plane_ref[...]
    first = jnp.bitwise_and(plane, outer - 1)
    plane = jnp.where(first > outer // 2, points - plane, plane)
    first = jnp.bitwise_and(plane, outer - 1)
    second = jnp.right_shift(plane, int(math.log2(outer)))
    pad = weights.shape[1]
    one_first = lax.broadcasted_iota(jnp.int32, (pad, planes), 0) == first
    one_second = (lax.broadcasted_iota(jnp.int32, (inner, planes), 0) == second).astype(jnp.float32)
    screen = screen_ref[...]
    scale = 1.0 / (points * planes)
    for p in range(k_rows):
        chosen = lax.broadcasted_iota(jnp.int32, screen.shape, 0) == table_ref[0, p]
        line = jnp.sum(jnp.where(chosen, screen, 0.0), axis=0, keepdims=True) * scale
        weights[p] = lax.dot_general(
            jnp.where(one_first, line, 0.0),
            one_second,
            NT,
            precision=lax.Precision.HIGHEST,
            preferred_element_type=jnp.float32,
        )

    def first_stage(p, kind):
        for u in range(NV):
            values = []
            for r in range(outer):
                lanes = slice(r * inner, (r + 1) * inner)
                values.append(left_f[2 * p + kind, u : u + 1, lanes] * right_f[kind, :, lanes])
            spots = pl.ds(pl.multiple_of((kind * NV + u) * NV, NV), NV)
            for f, (re, im) in enumerate(real_dft(values)):
                if f == 0:
                    stage[p, f, spots, :inner] = re
                    stage[p, f, spots, inner:] = jnp.zeros_like(re)
                    continue
                c = twist_ref[2 * f : 2 * f + 1, :]
                s = twist_ref[2 * f + 1 : 2 * f + 2, :]
                if im is None:
                    stage[p, f, spots, :inner] = re * c
                    stage[p, f, spots, inner:] = -(re * s)
                else:
                    stage[p, f, spots, :inner] = re * c + im * s
                    stage[p, f, spots, inner:] = im * c - re * s

    for i in range(n_kp):
        lanes = slice(i * part, (i + 1) * part)

        @pl.when(b != i)
        def _():
            remote(
                slabs.at[0, 0], cols.at[i], col_sems.at[0, 0], col_sems.at[1, i], a, kp_peer(1)
            ).wait_recv()

        right_f[:, :, lanes] = cols[i].astype(jnp.float32).reshape(2, NV, part)

    for p in range(k_rows):
        for i in range(n_kp):
            lanes = slice(i * part, (i + 1) * part)

            @pl.when(b != i)
            def _():
                remote(
                    waves_ref.at[p], rows.at[i, p], row_sems.at[0, 0, p], row_sems.at[1, i, p], a, kp_peer(1)
                ).wait_recv()

            left_f[2 * p : 2 * p + 2, :, lanes] = (
                rows[i, p].astype(jnp.float32).reshape(2, NV, part)
            )

        def step_of(kind, carry):
            first_stage(p, kind)
            return carry

        lax.fori_loop(0, 2, step_of, 0)
        high, low = split(stage[p].reshape(half * both, 2 * inner))
        spec = dot(high, dft_ref[0]) + dot(low, dft_ref[0]) + dot(high, dft_ref[1])
        left, right = [], []
        for f in range(half):
            line = weights[p, f : f + 1, :]
            line = jnp.concatenate([line, line], axis=1)
            val = spec[f * both : f * both + width]
            con = spec[f * both + width : (f + 1) * both] * line
            left.append(jnp.concatenate(split(val), axis=0))
            right.append(jnp.concatenate(split(con), axis=0))
        sums = dot(jnp.concatenate(left, axis=1), jnp.concatenate(right, axis=1), NT)
        total = sums[:width] + sums[width:]
        blocks[p * width : (p + 1) * width, :] = total + pltpu.roll(total, width, 1)

    grid = blocks[...]
    row_id = lax.broadcasted_iota(jnp.int32, grid.shape, 0)
    lane_id = lax.broadcasted_iota(jnp.int32, grid.shape, 1) // NC
    n_rows, n_lanes = grid.shape
    bit = 1
    while bit < NV:
        row_bit = jnp.bitwise_and(row_id, bit)
        lane_bit = jnp.bitwise_and(lane_id, bit)
        down = pltpu.roll(pltpu.roll(grid, n_rows - bit, 0), bit * NC, 1)
        up = pltpu.roll(pltpu.roll(grid, bit, 0), n_lanes - bit * NC, 1)
        grid = jnp.where(row_bit == lane_bit, grid, jnp.where(row_bit == 0, down, up))
        bit *= 2

    for step in range(1, n_ka):
        trial_copy(step, ka_peer(step)).wait_recv()
    for step in range(1, n_kp):
        probe_copy(step, kp_peer(step)).wait_recv()
    m_ka = trial_ref.shape[0]
    columns = m_ka * n_ka
    m_kp = probe_ref.shape[1]
    for i in range(n_ka):
        trial_f[i * m_ka : (i + 1) * m_ka, :] = trials[i].astype(jnp.float32)
    for i in range(n_kp):
        probe_f[:, i * m_kp : (i + 1) * m_kp, :] = probes[i].astype(jnp.float32)

    grid_high, grid_low = split(grid)
    trial = trial_f[...].astype(jnp.bfloat16)
    probe = probe_f[...].astype(jnp.bfloat16)
    forward = dot(trial, grid_high[:, :width], NT) + dot(trial, grid_low[:, :width], NT)
    backward = jnp.zeros((columns, 2 * width), jnp.float32)
    for p in range(k_rows):
        spots = slice(p * width, (p + 1) * width)
        backward += dot(probe[p], grid_high[spots]) + dot(probe[p], grid_low[spots])
    backward = backward[:, :width]
    for i in range(n_kp):
        app_send[i] = forward[i * m_kp : (i + 1) * m_kp]
    for i in range(n_ka):
        adj_send[i] = backward[i * m_ka : (i + 1) * m_ka]

    outs = []
    for step in range(1, n_kp):
        peer = kp_peer(step)
        outs.append(
            remote(app_send.at[peer], app_recv.at[b], app_sems.at[0, step], app_sems.at[1, b], a, peer)
        )
    for step in range(1, n_ka):
        peer = ka_peer(step)
        outs.append(
            remote(adj_send.at[peer], adj_recv.at[a], adj_sems.at[0, step], adj_sems.at[1, a], peer, b)
        )
    for copy in outs:
        copy.start()
    total = app_send[b]
    for step in range(1, n_kp):
        peer = kp_peer(step)
        remote(
            app_send.at[peer], app_recv.at[peer], app_sems.at[0, step], app_sems.at[1, peer], a, peer
        ).wait_recv()
        total = total + app_recv[peer]
    for p in range(k_rows):
        applied_ref[p] = total[:, p * width : (p + 1) * width]
    total = adj_send[a]
    for step in range(1, n_ka):
        peer = ka_peer(step)
        remote(
            adj_send.at[peer], adj_recv.at[peer], adj_sems.at[0, step], adj_sems.at[1, peer], peer, b
        ).wait_recv()
        total = total + adj_recv[peer]
    adjoint_ref[...] = total
    for copy in sends + outs:
        copy.wait_send()


def shards(n_ka, n_kp, waves, screen, pair_table, plane_map, trial, probe):
    k_rows, bands, part = waves.shape
    width = NV * NC
    points = part * n_kp
    outer = points // LANES
    half = outer // 2 + 1
    pad = -(-half // 8) * 8
    m_ka = trial.shape[2]
    m_kp = probe.shape[2]
    columns = m_ka * n_ka
    dft, twist = make_tables(outer, LANES)
    trial_t = trial.reshape(width, m_ka).T
    probe_t = probe.transpose(0, 2, 1)
    f32, bf16 = jnp.float32, jnp.bfloat16
    vmem = pl.BlockSpec(memory_space=pltpu.VMEM)
    smem = pl.BlockSpec(memory_space=pltpu.SMEM)
    dma = pltpu.SemaphoreType.DMA
    applied, adjoint = pl.pallas_call(
        functools.partial(kernel, n_ka, n_kp),
        out_shape=(
            jax.ShapeDtypeStruct((k_rows, m_kp, width), f32),
            jax.ShapeDtypeStruct((m_ka, width), f32),
        ),
        in_specs=[vmem, vmem, smem, vmem, vmem, vmem, vmem, vmem],
        out_specs=(vmem, vmem),
        scratch_shapes=[
            pltpu.VMEM((n_ka, k_rows, bands, part), bf16),
            pltpu.VMEM((n_kp, k_rows, bands, part), bf16),
            pltpu.VMEM((n_kp, bands, part), bf16),
            pltpu.VMEM((n_ka, m_ka, width), bf16),
            pltpu.VMEM((n_kp, k_rows, m_kp, width), bf16),
            pltpu.VMEM((2 * k_rows, NV, points), f32),
            pltpu.VMEM((2, NV, points), f32),
            pltpu.VMEM((k_rows, pad, LANES), f32),
            pltpu.VMEM((k_rows, half, 2 * width, 2 * LANES), f32),
            pltpu.VMEM((k_rows * width, 2 * width), f32),
            pltpu.VMEM((columns, width), f32),
            pltpu.VMEM((k_rows, columns, width), f32),
            pltpu.VMEM((n_kp, m_kp, k_rows * width), f32),
            pltpu.VMEM((n_kp, m_kp, k_rows * width), f32),
            pltpu.VMEM((n_ka, m_ka, width), f32),
            pltpu.VMEM((n_ka, m_ka, width), f32),
            dma((3,)),
            dma((2, n_ka)),
            dma((2, n_kp, k_rows)),
            dma((2, n_kp)),
            dma((2, n_ka)),
            dma((2, n_kp)),
            dma((2, n_kp)),
            dma((2, n_ka)),
        ],
        compiler_params=pltpu.CompilerParams(
            collective_id=0, has_side_effects=True, vmem_limit_bytes=60000 * 1024
        ),
    )(
        waves,
        screen,
        pair_table.T,
        plane_map.reshape(1, -1),
        trial_t,
        probe_t,
        jnp.asarray(dft),
        jnp.asarray(twist),
    )
    applied = applied.transpose(0, 2, 1)
    adjoint = adjoint.T.reshape(1, width, m_ka)
    return (applied, adjoint)


def solution(mesh):
    placed = (
        P("ka", None, "kp"),
        P(),
        P("ka", "kp"),
        P(),
        P("kp", None, "ka"),
        P("ka", None, "kp"),
    )
    return jax.shard_map(
        functools.partial(shards, mesh.shape["ka"], mesh.shape["kp"]),
        mesh=mesh,
        in_specs=placed,
        out_specs=(P("ka", None, "kp"), P("kp", None, "ka")),
        check_vma=False,
    )
```

```python
import functools
import math

import jax
import jax.numpy as jnp
import numpy as np
from jax import lax
from jax.experimental import pallas as pl
from jax.experimental.pallas import tpu as pltpu
from jax.sharding import PartitionSpec as P

NV = 8
NC = 8
CORES = 2
LANES = 128
MESH = pl.DeviceIdType.MESH
NT = (((1,), (1,)), ((), ()))
NN = (((1,), (0,)), ((), ()))


def split(value):
    high = value.astype(jnp.bfloat16)
    low = (value - high.astype(jnp.float32)).astype(jnp.bfloat16)
    return high, low


def dot(left, right, dims=NN):
    return lax.dot_general(left, right, dims, preferred_element_type=jnp.float32)


def real_dft(values):
    n = len(values)
    if n == 1:
        return [(values[0], None)]
    if n == 2:
        return [(values[0] + values[1], None), (values[0] - values[1], None)]
    even = real_dft(values[0::2])
    odd = real_dft(values[1::2])
    out = [None] * (n // 2 + 1)
    for k in range(n // 4 + 1):
        e_re, e_im = even[k]
        o_re, o_im = odd[k]
        if k == 0:
            out[0] = (e_re + o_re, None)
            out[n // 2] = (e_re - o_re, None)
            continue
        if 4 * k == n:
            out[k] = (e_re, -o_re)
            continue
        c = math.cos(2.0 * math.pi * k / n)
        s = math.sin(2.0 * math.pi * k / n)
        if 8 * k == n and o_im is not None:
            t_re, t_im = (o_re + o_im) * c, (o_im - o_re) * c
        elif o_im is None:
            t_re, t_im = o_re * c, o_re * (-s)
        else:
            t_re, t_im = o_re * c + o_im * s, o_im * c - o_re * s
        if e_im is None:
            out[k] = (e_re + t_re, t_im)
            out[n // 2 - k] = (e_re - t_re, t_im)
        else:
            out[k] = (e_re + t_re, e_im + t_im)
            out[n // 2 - k] = (e_re - t_re, t_im - e_im)
    return out


def make_tables(outer, inner):
    base = np.arange(inner)
    phase = 2.0 * np.pi * ((base[:, None] * base[None, :]) % inner) / inner
    cos, sin = np.cos(phase), np.sin(phase)
    full = np.block([[cos, -sin], [sin, cos]]).astype(np.float32)
    high = full.astype(jnp.bfloat16)
    low = (full - high.astype(np.float32)).astype(jnp.bfloat16)
    half = np.arange(outer // 2 + 1)
    phase = 2.0 * np.pi * (half[:, None] * base[None, :]) / (outer * inner)
    twist = np.stack([np.cos(phase), np.sin(phase)], axis=1).astype(np.float32)
    return np.stack([high, low]), twist.reshape(2 * (outer // 2 + 1), inner)


def kernel(
    n_ka,
    n_kp,
    waves_ref,
    screen_ref,
    table_ref,
    plane_ref,
    trial_ref,
    probe_ref,
    dft_ref,
    twist_ref,
    applied_ref,
    adjoint_ref,
    slabs,
    rows,
    cols,
    trials,
    probes,
    left_f,
    right_f,
    weights,
    stage,
    blocks,
    trial_f,
    probe_f,
    app_send,
    app_recv,
    adj_send,
    adj_recv,
    own_sems,
    slab_sems,
    row_sems,
    pass_sems,
    col_sems,
    trial_sems,
    probe_sems,
    app_sems,
    adj_sems,
):
    a = lax.axis_index("ka")
    b = lax.axis_index("kp")
    k_rows, bands, part = waves_ref.shape
    points = part * n_kp
    inner = LANES
    outer = points // inner
    half = outer // 2 + 1
    planes = plane_ref.shape[1]
    width = NV * NC
    both = 2 * width

    barrier = pltpu.get_barrier_semaphore()

    def greet(to_a, to_b):
        pl.semaphore_signal(barrier, inc=1, device_id=(to_a, to_b), device_id_type=MESH)

    def kp_peer(step):
        return lax.rem(b + step, n_kp)

    def ka_peer(step):
        return lax.rem(a + step, n_ka)

    for step in range(1, n_kp):
        greet(a, kp_peer(step))
    for step in range(1, n_ka):
        greet(ka_peer(step), b)
    own_slab = pltpu.make_async_copy(waves_ref, slabs.at[a], own_sems.at[0])
    own_slab.start()
    own_slab.wait()
    own_col = pltpu.make_async_copy(waves_ref, rows.at[b], own_sems.at[1])
    own_col.start()
    own_col.wait()
    trials[a] = trial_ref[...]
    probes[b] = probe_ref[...]
    plane = plane_ref[...]
    first = jnp.bitwise_and(plane, outer - 1)
    plane = jnp.where(first > outer // 2, points - plane, plane)
    first = jnp.bitwise_and(plane, outer - 1)
    second = jnp.right_shift(plane, int(math.log2(outer)))
    pad = weights.shape[1]
    one_first = lax.broadcasted_iota(jnp.int32, (pad, planes), 0) == first
    one_second = (lax.broadcasted_iota(jnp.int32, (inner, planes), 0) == second).astype(jnp.float32)
    screen = screen_ref[...]
    scale = 1.0 / (points * planes)
    for p in range(k_rows):
        chosen = lax.broadcasted_iota(jnp.int32, screen.shape, 0) == table_ref[0, p]
        line = jnp.sum(jnp.where(chosen, screen, 0.0), axis=0, keepdims=True) * scale
        weights[p] = lax.dot_general(
            jnp.where(one_first, line, 0.0),
            one_second,
            NT,
            precision=lax.Precision.HIGHEST,
            preferred_element_type=jnp.float32,
        )

    pl.semaphore_wait(barrier, (n_kp - 1) + (n_ka - 1))

    def remote(src, dst, send, recv, to_a, to_b):
        return pltpu.make_async_remote_copy(
            src_ref=src,
            dst_ref=dst,
            send_sem=send,
            recv_sem=recv,
            device_id=(to_a, to_b),
            device_id_type=MESH,
        )

    def slab_copy(step, slot):
        return remote(
            waves_ref, slabs.at[slot], slab_sems.at[0, step], slab_sems.at[1, slot], ka_peer(step), b
        )

    chips = n_kp // CORES
    core = lax.rem(b, CORES)
    partner = b + 1 - 2 * core

    def same_core(step):
        return lax.rem(b + step * CORES, n_kp)

    def row_copy(step, slot):
        return remote(
            waves_ref, rows.at[slot], row_sems.at[0, step], row_sems.at[1, slot], a, same_core(step)
        )

    def pass_copy(step, slot):
        return remote(
            waves_ref if step == 0 else rows.at[slot],
            rows.at[slot],
            pass_sems.at[step],
            row_sems.at[1, slot],
            a,
            partner,
        )

    def col_copy(index, peer, slot):
        return remote(
            slabs.at[peer // k_rows, lax.rem(peer, k_rows)],
            cols.at[slot],
            col_sems.at[0, index],
            col_sems.at[1, slot],
            a,
            peer,
        )

    def trial_copy(step, slot):
        return remote(
            trial_ref, trials.at[slot], trial_sems.at[0, step], trial_sems.at[1, slot], ka_peer(step), b
        )

    def probe_copy(step, slot):
        return remote(
            probe_ref, probes.at[slot], probe_sems.at[0, step], probe_sems.at[1, slot], a, kp_peer(step)
        )

    sends = []

    def send(copy):
        copy.start()
        sends.append(copy)

    for step in range(1, n_ka):
        send(slab_copy(step, a))
    for step in range(1, chips):
        send(row_copy(step, b))
    send(pass_copy(0, b))
    guarded = []
    for step in range(n_ka):
        owner = ka_peer(step)
        if step:
            slab_copy(step, owner).wait_recv()
        for t in range(k_rows):
            peer = owner * k_rows + t
            copy = col_copy(step * k_rows + t, peer, b)
            guarded.append((peer, copy))
            pl.when(peer != b)(copy.start)
    for step in range(1, n_ka):
        send(trial_copy(step, a))
    for step in range(1, n_kp):
        send(probe_copy(step, b))
    for step in range(1, chips):
        slot = same_core(step)
        row_copy(step, slot).wait_recv()
        send(pass_copy(step, slot))
    own_col = pltpu.make_async_copy(
        slabs.at[b // k_rows, lax.rem(b, k_rows)], cols.at[b], own_sems.at[2]
    )
    own_col.start()
    own_col.wait()

    def first_stage(p, kind):
        for u in range(NV):
            values = []
            for r in range(outer):
                lanes = slice(r * inner, (r + 1) * inner)
                values.append(left_f[2 * p + kind, u : u + 1, lanes] * right_f[kind, :, lanes])
            spots = pl.ds(pl.multiple_of((kind * NV + u) * NV, NV), NV)
            for f, (re, im) in enumerate(real_dft(values)):
                if f == 0:
                    stage[p, f, spots, :inner] = re
                    stage[p, f, spots, inner:] = jnp.zeros_like(re)
                    continue
                c = twist_ref[2 * f : 2 * f + 1, :]
                s = twist_ref[2 * f + 1 : 2 * f + 2, :]
                if im is None:
                    stage[p, f, spots, :inner] = re * c
                    stage[p, f, spots, inner:] = -(re * s)
                else:
                    stage[p, f, spots, :inner] = re * c + im * s
                    stage[p, f, spots, inner:] = im * c - re * s

    for i in range(n_kp):
        lanes = slice(i * part, (i + 1) * part)

        @pl.when(core != i % CORES)
        def _():
            pass_copy(1, i).wait_recv()

        for p in range(k_rows):
            left_f[2 * p : 2 * p + 2, :, lanes] = (
                rows[i, p].astype(jnp.float32).reshape(2, NV, part)
            )

    for i in range(n_kp):
        lanes = slice(i * part, (i + 1) * part)

        @pl.when(b != i)
        def _():
            col_copy(0, kp_peer(1), i).wait_recv()

        right_f[:, :, lanes] = cols[i].astype(jnp.float32).reshape(2, NV, part)

    for p in range(k_rows):
        def step_of(kind, carry):
            first_stage(p, kind)
            return carry

        lax.fori_loop(0, 2, step_of, 0)
        high, low = split(stage[p].reshape(half * both, 2 * inner))
        spec = dot(high, dft_ref[0]) + dot(low, dft_ref[0]) + dot(high, dft_ref[1])
        left, right = [], []
        for f in range(half):
            line = weights[p, f : f + 1, :]
            line = jnp.concatenate([line, line], axis=1)
            val = spec[f * both : f * both + width]
            con = spec[f * both + width : (f + 1) * both] * line
            left.append(jnp.concatenate(split(val), axis=0))
            right.append(jnp.concatenate(split(con), axis=0))
        sums = dot(jnp.concatenate(left, axis=1), jnp.concatenate(right, axis=1), NT)
        total = sums[:width] + sums[width:]
        blocks[p * width : (p + 1) * width, :] = total + pltpu.roll(total, width, 1)

    grid = blocks[...]
    row_id = lax.broadcasted_iota(jnp.int32, grid.shape, 0)
    lane_id = lax.broadcasted_iota(jnp.int32, grid.shape, 1) // NC
    n_rows, n_lanes = grid.shape
    bit = 1
    while bit < NV:
        row_bit = jnp.bitwise_and(row_id, bit)
        lane_bit = jnp.bitwise_and(lane_id, bit)
        down = pltpu.roll(pltpu.roll(grid, n_rows - bit, 0), bit * NC, 1)
        up = pltpu.roll(pltpu.roll(grid, bit, 0), n_lanes - bit * NC, 1)
        grid = jnp.where(row_bit == lane_bit, grid, jnp.where(row_bit == 0, down, up))
        bit *= 2

    for step in range(1, n_ka):
        trial_copy(step, ka_peer(step)).wait_recv()
    for step in range(1, n_kp):
        probe_copy(step, kp_peer(step)).wait_recv()
    m_ka = trial_ref.shape[0]
    columns = m_ka * n_ka
    m_kp = probe_ref.shape[1]
    for i in range(n_ka):
        trial_f[i * m_ka : (i + 1) * m_ka, :] = trials[i].astype(jnp.float32)
    for i in range(n_kp):
        probe_f[:, i * m_kp : (i + 1) * m_kp, :] = probes[i].astype(jnp.float32)

    grid_high, grid_low = split(grid)
    trial = trial_f[...].astype(jnp.bfloat16)
    probe = probe_f[...].astype(jnp.bfloat16)
    forward = dot(trial, grid_high[:, :width], NT) + dot(trial, grid_low[:, :width], NT)
    backward = jnp.zeros((columns, 2 * width), jnp.float32)
    for p in range(k_rows):
        spots = slice(p * width, (p + 1) * width)
        backward += dot(probe[p], grid_high[spots]) + dot(probe[p], grid_low[spots])
    backward = backward[:, :width]
    for i in range(n_kp):
        app_send[i] = forward[i * m_kp : (i + 1) * m_kp]
    for i in range(n_ka):
        adj_send[i] = backward[i * m_ka : (i + 1) * m_ka]

    outs = []
    for step in range(1, n_kp):
        peer = kp_peer(step)
        outs.append(
            remote(app_send.at[peer], app_recv.at[b], app_sems.at[0, step], app_sems.at[1, b], a, peer)
        )
    for step in range(1, n_ka):
        peer = ka_peer(step)
        outs.append(
            remote(adj_send.at[peer], adj_recv.at[a], adj_sems.at[0, step], adj_sems.at[1, a], peer, b)
        )
    for copy in outs:
        copy.start()
    total = app_send[b]
    for step in range(1, n_kp):
        peer = kp_peer(step)
        remote(
            app_send.at[peer], app_recv.at[peer], app_sems.at[0, step], app_sems.at[1, peer], a, peer
        ).wait_recv()
        total = total + app_recv[peer]
    for p in range(k_rows):
        applied_ref[p] = total[:, p * width : (p + 1) * width]
    total = adj_send[a]
    for step in range(1, n_ka):
        peer = ka_peer(step)
        remote(
            adj_send.at[peer], adj_recv.at[peer], adj_sems.at[0, step], adj_sems.at[1, peer], peer, b
        ).wait_recv()
        total = total + adj_recv[peer]
    adjoint_ref[...] = total
    for copy in sends + outs:
        copy.wait_send()
    for peer, copy in guarded:
        pl.when(peer != b)(copy.wait_send)


def shards(n_ka, n_kp, waves, screen, pair_table, plane_map, trial, probe):
    k_rows, bands, part = waves.shape
    width = NV * NC
    points = part * n_kp
    outer = points // LANES
    half = outer // 2 + 1
    pad = -(-half // 8) * 8
    m_ka = trial.shape[2]
    m_kp = probe.shape[2]
    columns = m_ka * n_ka
    dft, twist = make_tables(outer, LANES)
    trial_t = trial.reshape(width, m_ka).T
    probe_t = probe.transpose(0, 2, 1)
    f32, bf16 = jnp.float32, jnp.bfloat16
    vmem = pl.BlockSpec(memory_space=pltpu.VMEM)
    smem = pl.BlockSpec(memory_space=pltpu.SMEM)
    dma = pltpu.SemaphoreType.DMA
    applied, adjoint = pl.pallas_call(
        functools.partial(kernel, n_ka, n_kp),
        out_shape=(
            jax.ShapeDtypeStruct((k_rows, m_kp, width), f32),
            jax.ShapeDtypeStruct((m_ka, width), f32),
        ),
        in_specs=[vmem, vmem, smem, vmem, vmem, vmem, vmem, vmem],
        out_specs=(vmem, vmem),
        scratch_shapes=[
            pltpu.VMEM((n_ka, k_rows, bands, part), bf16),
            pltpu.VMEM((n_kp, k_rows, bands, part), bf16),
            pltpu.VMEM((n_kp, bands, part), bf16),
            pltpu.VMEM((n_ka, m_ka, width), bf16),
            pltpu.VMEM((n_kp, k_rows, m_kp, width), bf16),
            pltpu.VMEM((2 * k_rows, NV, points), f32),
            pltpu.VMEM((2, NV, points), f32),
            pltpu.VMEM((k_rows, pad, LANES), f32),
            pltpu.VMEM((k_rows, half, 2 * width, 2 * LANES), f32),
            pltpu.VMEM((k_rows * width, 2 * width), f32),
            pltpu.VMEM((columns, width), f32),
            pltpu.VMEM((k_rows, columns, width), f32),
            pltpu.VMEM((n_kp, m_kp, k_rows * width), f32),
            pltpu.VMEM((n_kp, m_kp, k_rows * width), f32),
            pltpu.VMEM((n_ka, m_ka, width), f32),
            pltpu.VMEM((n_ka, m_ka, width), f32),
            dma((3,)),
            dma((2, n_ka)),
            dma((2, n_kp)),
            dma((n_kp // CORES,)),
            dma((2, n_kp)),
            dma((2, n_ka)),
            dma((2, n_kp)),
            dma((2, n_kp)),
            dma((2, n_ka)),
        ],
        compiler_params=pltpu.CompilerParams(
            collective_id=0, has_side_effects=True, vmem_limit_bytes=60000 * 1024
        ),
    )(
        waves,
        screen,
        pair_table.T,
        plane_map.reshape(1, -1),
        trial_t,
        probe_t,
        jnp.asarray(dft),
        jnp.asarray(twist),
    )
    applied = applied.transpose(0, 2, 1)
    adjoint = adjoint.T.reshape(1, width, m_ka)
    return (applied, adjoint)


def solution(mesh):
    placed = (
        P("ka", None, "kp"),
        P(),
        P("ka", "kp"),
        P(),
        P("kp", None, "ka"),
        P("ka", None, "kp"),
    )
    return jax.shard_map(
        functools.partial(shards, mesh.shape["ka"], mesh.shape["kp"]),
        mesh=mesh,
        in_specs=placed,
        out_specs=(P("ka", None, "kp"), P("kp", None, "ka")),
        check_vma=False,
    )
```

```python
import functools
import math

import jax
import jax.numpy as jnp
import numpy as np
from jax import lax
from jax.experimental import pallas as pl
from jax.experimental.pallas import tpu as pltpu
from jax.sharding import PartitionSpec as P

NV = 8
NC = 8
CORES = 2
LANES = 128
MESH = pl.DeviceIdType.MESH
NT = (((1,), (1,)), ((), ()))
NN = (((1,), (0,)), ((), ()))


def split(value):
    high = value.astype(jnp.bfloat16)
    low = (value - high.astype(jnp.float32)).astype(jnp.bfloat16)
    return high, low


def dot(left, right, dims=NN):
    return lax.dot_general(left, right, dims, preferred_element_type=jnp.float32)


def real_dft(values):
    n = len(values)
    if n == 1:
        return [(values[0], None)]
    if n == 2:
        return [(values[0] + values[1], None), (values[0] - values[1], None)]
    even = real_dft(values[0::2])
    odd = real_dft(values[1::2])
    out = [None] * (n // 2 + 1)
    for k in range(n // 4 + 1):
        e_re, e_im = even[k]
        o_re, o_im = odd[k]
        if k == 0:
            out[0] = (e_re + o_re, None)
            out[n // 2] = (e_re - o_re, None)
            continue
        if 4 * k == n:
            out[k] = (e_re, -o_re)
            continue
        c = math.cos(2.0 * math.pi * k / n)
        s = math.sin(2.0 * math.pi * k / n)
        if 8 * k == n and o_im is not None:
            t_re, t_im = (o_re + o_im) * c, (o_im - o_re) * c
        elif o_im is None:
            t_re, t_im = o_re * c, o_re * (-s)
        else:
            t_re, t_im = o_re * c + o_im * s, o_im * c - o_re * s
        if e_im is None:
            out[k] = (e_re + t_re, t_im)
            out[n // 2 - k] = (e_re - t_re, t_im)
        else:
            out[k] = (e_re + t_re, e_im + t_im)
            out[n // 2 - k] = (e_re - t_re, t_im - e_im)
    return out


def make_tables(outer, inner):
    base = np.arange(inner)
    phase = 2.0 * np.pi * ((base[:, None] * base[None, :]) % inner) / inner
    cos, sin = np.cos(phase), np.sin(phase)
    full = np.block([[cos, -sin], [sin, cos]]).astype(np.float32)
    high = full.astype(jnp.bfloat16)
    low = (full - high.astype(np.float32)).astype(jnp.bfloat16)
    half = np.arange(outer // 2 + 1)
    phase = 2.0 * np.pi * (half[:, None] * base[None, :]) / (outer * inner)
    twist = np.stack([np.cos(phase), np.sin(phase)], axis=1).astype(np.float32)
    return np.stack([high, low]), twist.reshape(2 * (outer // 2 + 1), inner)


def kernel(
    n_ka,
    n_kp,
    waves_ref,
    screen_ref,
    table_ref,
    plane_ref,
    trial_ref,
    probe_ref,
    dft_ref,
    twist_ref,
    out_ref,
    slabs,
    rows,
    cols,
    trials,
    probes,
    left_f,
    right_f,
    weights,
    stage,
    blocks,
    trial_f,
    probe_f,
    app_send,
    app_recv,
    adj_send,
    adj_recv,
    own_sems,
    slab_sems,
    row_sems,
    pass_sems,
    col_sems,
    trial_sems,
    probe_sems,
    app_sems,
    adj_sems,
):
    a = lax.axis_index("ka")
    b = lax.axis_index("kp")
    k_rows, bands, part = waves_ref.shape
    points = part * n_kp
    inner = LANES
    outer = points // inner
    half = outer // 2 + 1
    planes = plane_ref.shape[1]
    width = NV * NC
    both = 2 * width

    barrier = pltpu.get_barrier_semaphore()

    def greet(to_a, to_b):
        pl.semaphore_signal(barrier, inc=1, device_id=(to_a, to_b), device_id_type=MESH)

    def kp_peer(step):
        return lax.rem(b + step, n_kp)

    def ka_peer(step):
        return lax.rem(a + step, n_ka)

    for step in range(1, n_kp):
        greet(a, kp_peer(step))
    for step in range(1, n_ka):
        greet(ka_peer(step), b)
    own_slab = pltpu.make_async_copy(waves_ref, slabs.at[a], own_sems.at[0])
    own_slab.start()
    own_slab.wait()
    own_col = pltpu.make_async_copy(waves_ref, rows.at[b], own_sems.at[1])
    own_col.start()
    own_col.wait()
    trials[a] = trial_ref[...]
    probes[b] = probe_ref[...]
    plane = plane_ref[...]
    first = jnp.bitwise_and(plane, outer - 1)
    plane = jnp.where(first > outer // 2, points - plane, plane)
    first = jnp.bitwise_and(plane, outer - 1)
    second = jnp.right_shift(plane, int(math.log2(outer)))
    pad = weights.shape[1]
    one_first = lax.broadcasted_iota(jnp.int32, (pad, planes), 0) == first
    one_second = (lax.broadcasted_iota(jnp.int32, (inner, planes), 0) == second).astype(jnp.float32)
    screen = screen_ref[...]
    scale = 1.0 / (points * planes)
    for p in range(k_rows):
        chosen = lax.broadcasted_iota(jnp.int32, screen.shape, 0) == table_ref[0, p]
        line = jnp.sum(jnp.where(chosen, screen, 0.0), axis=0, keepdims=True) * scale
        weights[p] = lax.dot_general(
            jnp.where(one_first, line, 0.0),
            one_second,
            NT,
            precision=lax.Precision.HIGHEST,
            preferred_element_type=jnp.float32,
        )

    pl.semaphore_wait(barrier, (n_kp - 1) + (n_ka - 1))

    def remote(src, dst, send, recv, to_a, to_b):
        return pltpu.make_async_remote_copy(
            src_ref=src,
            dst_ref=dst,
            send_sem=send,
            recv_sem=recv,
            device_id=(to_a, to_b),
            device_id_type=MESH,
        )

    def slab_copy(step, slot):
        return remote(
            waves_ref, slabs.at[slot], slab_sems.at[0, step], slab_sems.at[1, slot], ka_peer(step), b
        )

    chips = n_kp // CORES
    core = lax.rem(b, CORES)
    partner = b + 1 - 2 * core

    def same_core(step):
        return lax.rem(b + step * CORES, n_kp)

    def row_copy(step, slot):
        return remote(
            waves_ref, rows.at[slot], row_sems.at[0, step], row_sems.at[1, slot], a, same_core(step)
        )

    def pass_copy(step, slot):
        return remote(
            waves_ref if step == 0 else rows.at[slot],
            rows.at[slot],
            pass_sems.at[step],
            row_sems.at[1, slot],
            a,
            partner,
        )

    def col_copy(index, peer, slot):
        return remote(
            slabs.at[peer // k_rows, lax.rem(peer, k_rows)],
            cols.at[slot],
            col_sems.at[0, index],
            col_sems.at[1, slot],
            a,
            peer,
        )

    def trial_copy(step, slot):
        return remote(
            trial_ref, trials.at[slot], trial_sems.at[0, step], trial_sems.at[1, slot], ka_peer(step), b
        )

    def probe_copy(step, slot):
        return remote(
            probe_ref, probes.at[slot], probe_sems.at[0, step], probe_sems.at[1, slot], a, kp_peer(step)
        )

    sends = []

    def send(copy):
        copy.start()
        sends.append(copy)

    for step in range(1, n_ka):
        send(slab_copy(step, a))
    for step in range(1, chips):
        send(row_copy(step, b))
    send(pass_copy(0, b))
    guarded = []
    for step in range(n_ka):
        owner = ka_peer(step)
        if step:
            slab_copy(step, owner).wait_recv()
        for t in range(k_rows):
            peer = owner * k_rows + t
            copy = col_copy(step * k_rows + t, peer, b)
            guarded.append((peer, copy))
            pl.when(peer != b)(copy.start)
    for step in range(1, n_ka):
        send(trial_copy(step, a))
    for step in range(1, n_kp):
        send(probe_copy(step, b))
    for step in range(1, chips):
        slot = same_core(step)
        row_copy(step, slot).wait_recv()
        send(pass_copy(step, slot))
    own_col = pltpu.make_async_copy(
        slabs.at[b // k_rows, lax.rem(b, k_rows)], cols.at[b], own_sems.at[2]
    )
    own_col.start()
    own_col.wait()

    def first_stage(p, kind):
        for u in range(NV):
            values = []
            for r in range(outer):
                lanes = slice(r * inner, (r + 1) * inner)
                values.append(left_f[2 * p + kind, u : u + 1, lanes] * right_f[kind, :, lanes])
            spots = pl.ds(pl.multiple_of((kind * NV + u) * NV, NV), NV)
            for f, (re, im) in enumerate(real_dft(values)):
                if f == 0:
                    stage[p, f, spots, :inner] = re
                    stage[p, f, spots, inner:] = jnp.zeros_like(re)
                    continue
                c = twist_ref[2 * f : 2 * f + 1, :]
                s = twist_ref[2 * f + 1 : 2 * f + 2, :]
                if im is None:
                    stage[p, f, spots, :inner] = re * c
                    stage[p, f, spots, inner:] = -(re * s)
                else:
                    stage[p, f, spots, :inner] = re * c + im * s
                    stage[p, f, spots, inner:] = im * c - re * s

    for i in range(n_kp):
        lanes = slice(i * part, (i + 1) * part)

        @pl.when(core != i % CORES)
        def _():
            pass_copy(1, i).wait_recv()

        for p in range(k_rows):
            left_f[2 * p : 2 * p + 2, :, lanes] = (
                rows[i, p].astype(jnp.float32).reshape(2, NV, part)
            )

    for i in range(n_kp):
        lanes = slice(i * part, (i + 1) * part)

        @pl.when(b != i)
        def _():
            col_copy(0, kp_peer(1), i).wait_recv()

        right_f[:, :, lanes] = cols[i].astype(jnp.float32).reshape(2, NV, part)

    for p in range(k_rows):
        def step_of(kind, carry):
            first_stage(p, kind)
            return carry

        lax.fori_loop(0, 2, step_of, 0)
        high, low = split(stage[p].reshape(half * both, 2 * inner))
        spec = dot(high, dft_ref[0]) + dot(low, dft_ref[0]) + dot(high, dft_ref[1])
        left, right = [], []
        for f in range(half):
            line = weights[p, f : f + 1, :]
            line = jnp.concatenate([line, line], axis=1)
            val = spec[f * both : f * both + width]
            con = spec[f * both + width : (f + 1) * both] * line
            left.append(jnp.concatenate(split(val), axis=0))
            right.append(jnp.concatenate(split(con), axis=0))
        sums = dot(jnp.concatenate(left, axis=1), jnp.concatenate(right, axis=1), NT)
        total = sums[:width] + sums[width:]
        blocks[p * width : (p + 1) * width, :] = total + pltpu.roll(total, width, 1)

    grid = blocks[...]
    row_id = lax.broadcasted_iota(jnp.int32, grid.shape, 0)
    lane_id = lax.broadcasted_iota(jnp.int32, grid.shape, 1) // NC
    n_rows, n_lanes = grid.shape
    bit = 1
    while bit < NV:
        row_bit = jnp.bitwise_and(row_id, bit)
        lane_bit = jnp.bitwise_and(lane_id, bit)
        down = pltpu.roll(pltpu.roll(grid, n_rows - bit, 0), bit * NC, 1)
        up = pltpu.roll(pltpu.roll(grid, bit, 0), n_lanes - bit * NC, 1)
        grid = jnp.where(row_bit == lane_bit, grid, jnp.where(row_bit == 0, down, up))
        bit *= 2

    for step in range(1, n_ka):
        trial_copy(step, ka_peer(step)).wait_recv()
    for step in range(1, n_kp):
        probe_copy(step, kp_peer(step)).wait_recv()
    m_ka = trial_ref.shape[0]
    columns = m_ka * n_ka
    m_kp = probe_ref.shape[1]
    for i in range(n_ka):
        trial_f[i * m_ka : (i + 1) * m_ka, :] = trials[i].astype(jnp.float32)
    for i in range(n_kp):
        probe_f[:, i * m_kp : (i + 1) * m_kp, :] = probes[i].astype(jnp.float32)

    grid_high, grid_low = split(grid)
    trial = trial_f[...].astype(jnp.bfloat16)
    probe = probe_f[...].astype(jnp.bfloat16)
    forward = dot(trial, grid_high[:, :width], NT) + dot(trial, grid_low[:, :width], NT)
    backward = jnp.zeros((columns, 2 * width), jnp.float32)
    for p in range(k_rows):
        spots = slice(p * width, (p + 1) * width)
        backward += dot(probe[p], grid_high[spots]) + dot(probe[p], grid_low[spots])
    backward = backward[:, :width]
    for i in range(n_kp):
        app_send[i] = forward[i * m_kp : (i + 1) * m_kp]
    for i in range(n_ka):
        adj_send[i] = backward[i * m_ka : (i + 1) * m_ka]

    outs = []
    for step in range(1, n_kp):
        peer = kp_peer(step)
        outs.append(
            remote(app_send.at[peer], app_recv.at[b], app_sems.at[0, step], app_sems.at[1, b], a, peer)
        )
    for step in range(1, n_ka):
        peer = ka_peer(step)
        outs.append(
            remote(adj_send.at[peer], adj_recv.at[a], adj_sems.at[0, step], adj_sems.at[1, a], peer, b)
        )
    for copy in outs:
        copy.start()
    total = app_send[b]
    for step in range(1, n_kp):
        peer = kp_peer(step)
        remote(
            app_send.at[peer], app_recv.at[peer], app_sems.at[0, step], app_sems.at[1, peer], a, peer
        ).wait_recv()
        total = total + app_recv[peer]
    for p in range(k_rows):
        out_ref[p * m_kp : (p + 1) * m_kp, :] = total[:, p * width : (p + 1) * width]
    total = adj_send[a]
    for step in range(1, n_ka):
        peer = ka_peer(step)
        remote(
            adj_send.at[peer], adj_recv.at[peer], adj_sems.at[0, step], adj_sems.at[1, peer], peer, b
        ).wait_recv()
        total = total + adj_recv[peer]
    out_ref[k_rows * m_kp :, :] = total
    for copy in sends + outs:
        copy.wait_send()
    for peer, copy in guarded:
        pl.when(peer != b)(copy.wait_send)


def shards(n_ka, n_kp, waves, screen, pair_table, plane_map, trial, probe):
    k_rows, bands, part = waves.shape
    width = NV * NC
    points = part * n_kp
    outer = points // LANES
    half = outer // 2 + 1
    pad = -(-half // 8) * 8
    m_ka = trial.shape[2]
    m_kp = probe.shape[2]
    columns = m_ka * n_ka
    dft, twist = make_tables(outer, LANES)
    trial_t = trial.reshape(width, m_ka).T
    probe_t = probe.transpose(0, 2, 1)
    f32, bf16 = jnp.float32, jnp.bfloat16
    vmem = pl.BlockSpec(memory_space=pltpu.VMEM)
    smem = pl.BlockSpec(memory_space=pltpu.SMEM)
    dma = pltpu.SemaphoreType.DMA
    out = pl.pallas_call(
        functools.partial(kernel, n_ka, n_kp),
        out_shape=jax.ShapeDtypeStruct((k_rows * m_kp + m_ka, width), f32),
        in_specs=[vmem, vmem, smem, vmem, vmem, vmem, vmem, vmem],
        out_specs=vmem,
        scratch_shapes=[
            pltpu.VMEM((n_ka, k_rows, bands, part), bf16),
            pltpu.VMEM((n_kp, k_rows, bands, part), bf16),
            pltpu.VMEM((n_kp, bands, part), bf16),
            pltpu.VMEM((n_ka, m_ka, width), bf16),
            pltpu.VMEM((n_kp, k_rows, m_kp, width), bf16),
            pltpu.VMEM((2 * k_rows, NV, points), f32),
            pltpu.VMEM((2, NV, points), f32),
            pltpu.VMEM((k_rows, pad, LANES), f32),
            pltpu.VMEM((k_rows, half, 2 * width, 2 * LANES), f32),
            pltpu.VMEM((k_rows * width, 2 * width), f32),
            pltpu.VMEM((columns, width), f32),
            pltpu.VMEM((k_rows, columns, width), f32),
            pltpu.VMEM((n_kp, m_kp, k_rows * width), f32),
            pltpu.VMEM((n_kp, m_kp, k_rows * width), f32),
            pltpu.VMEM((n_ka, m_ka, width), f32),
            pltpu.VMEM((n_ka, m_ka, width), f32),
            dma((3,)),
            dma((2, n_ka)),
            dma((2, n_kp)),
            dma((n_kp // CORES,)),
            dma((2, n_kp)),
            dma((2, n_ka)),
            dma((2, n_kp)),
            dma((2, n_kp)),
            dma((2, n_ka)),
        ],
        compiler_params=pltpu.CompilerParams(
            collective_id=0, has_side_effects=True, vmem_limit_bytes=60000 * 1024
        ),
    )(
        waves,
        screen,
        pair_table.T,
        plane_map.reshape(1, -1),
        trial_t,
        probe_t,
        jnp.asarray(dft),
        jnp.asarray(twist),
    )
    applied = out[: k_rows * m_kp].reshape(k_rows, m_kp, width).transpose(0, 2, 1)
    adjoint = out[k_rows * m_kp :].T.reshape(1, width, m_ka)
    return (applied, adjoint)


def solution(mesh):
    placed = (
        P("ka", None, "kp"),
        P(),
        P("ka", "kp"),
        P(),
        P("kp", None, "ka"),
        P("ka", None, "kp"),
    )
    return jax.shard_map(
        functools.partial(shards, mesh.shape["ka"], mesh.shape["kp"]),
        mesh=mesh,
        in_specs=placed,
        out_specs=(P("ka", None, "kp"), P("kp", None, "ka")),
        check_vma=False,
    )
```
